32 devices in a mesh: group: 2 (over y), seq: 4 (over z), expert: 2 (over x), fsdp: 2 (over core).
Axes of the slice: x: 2, y: 2, z: 4, core: 2. Of those that a mesh axis runs over, the one named last changes fastest.
Arguments:
- queries: bfloat16 [4096, 3072], P(('group', 'seq'), ('expert', 'fsdp')), parts along dimension 0, may hold values from -1000 to 1000
- keys: bfloat16 [4096, 3072], P(('group', 'seq'), ('expert', 'fsdp')), parts along dimension 0, may hold values from -10 to 10
- values: bfloat16 [4096, 3072], P(('group', 'seq'), ('expert', 'fsdp')), parts along dimension 0, may hold values from -12 to 12
- tokens: bfloat16 [4096, 3072], P(('group', 'seq', 'expert', 'fsdp')), parts along dimension 0, may hold values from -200 to 200
- modulation: float32 [6, 3072], P('group'), parts along dimension 0, may hold values from -3 to 3
- out_weight: bfloat16 [3072, 3072], P(('expert', 'fsdp')), may hold values from -0.21875 to 0.21875
- fc_in: bfloat16 [8, 1536, 3072], P(('seq', 'expert'), 'fsdp'), may hold values from -0.109375 to 0.109375
- fc_out: bfloat16 [8, 1536, 3072], P(('seq', 'expert'), 'fsdp'), may hold values from -0.15625 to 0.15625
- expert_ids: int32 [4096, 2], P(('group', 'seq', 'expert', 'fsdp')), parts along dimension 0, may hold values from 0 to 7, all different within a row; in each aligned block of 128 rows (0 to 127, 128 to 255, ...) at most 64 rows name the same one
- gate_weights: float32 [4096, 2], P(('group', 'seq', 'expert', 'fsdp')), parts along dimension 0, may hold values from 0.1 to 1
Outputs:
- layer_out: bfloat16 [4096, 3072], P(('group', 'seq', 'expert', 'fsdp')), parts along dimension 0
The draws below stay inside these ranges and needn't reach their ends.
There are 2 independent parts, one for each index of `group`. The reference program is written for one: setup_inputs(seed, part) draws one part's arguments, and reference() takes and returns one part's arrays. A program takes and returns all parts, laid end to end along the dimension named above; an argument that names none is the same for every part. Nothing has to cross between parts.
Inputs may be any that keep to these rules, and one draw needn't show every extreme that they name: `expert_ids`: in each aligned block of 128 tokens (the rows of one device) no expert is named by more than 64 tokens; a token's 2 experts differ.
All inputs are finite; a program needn't handle non-finite values.
Results may differ from the reference program's by a relative error of at most 0.014.
Values may be sent and summed in bfloat16 or wider, within the bound.
No kernel may reach another device: no remote copies, remote signals or barrier semaphores. Data moves between devices by JAX's collectives and lax.ppermute only.
A program may use at most 192 MiB of HBM per device.

```python
import math
import jax
import jax.numpy as jnp
import numpy as np
from jax import lax

D = 3072
HEADS = 24
HEAD_DIM = 128
H = 1536
TOP = 2
LENGTH = 2048
TOK_DEV = 128
EXPERTS = 8
CAP = 64


def twin_fields(key):
    head_scales = jnp.exp(jax.random.uniform(jax.random.fold_in(key, 105), (HEADS,), jnp.float32, math.log(1.5), math.log(4.5)))
    column_scales = jnp.repeat(head_scales, HEAD_DIM)
    query_all = jax.random.normal(jax.random.fold_in(key, 101), (LENGTH, D), jnp.float32) * column_scales[None, :]
    key_all = jax.random.normal(jax.random.fold_in(key, 102), (LENGTH, D), jnp.float32)
    return (query_all, key_all)


def draw_queries(key, part):
    return twin_fields(key)[0].astype(jnp.bfloat16)


def draw_keys(key, part):
    return twin_fields(key)[1].astype(jnp.bfloat16)


def draw_tokens(key, part):
    stream = jax.random.normal(jax.random.fold_in(key, 201), (LENGTH, D), jnp.float32)
    return stream.astype(jnp.bfloat16)


def block_scale(stream_key, dims, split, smallest, largest):
    factor_of, own = 1.0, jax.random.fold_in(stream_key, 6)
    for axis_at, blocks in split:
        heights = jnp.exp(jax.random.uniform(jax.random.fold_in(own, axis_at), (blocks,), jnp.float32, smallest / len(split), largest / len(split)))
        factor_of = factor_of * jnp.repeat(heights, dims[axis_at] // blocks).reshape([-1 if axis == axis_at else 1 for axis in range(len(dims))])
    return factor_of


def deal_out(key, own, number, rows, amount, top, limit, slope):
    ranking = jax.random.permutation(key, amount)
    crowded, ordinary = load_shares(amount, rows * top, limit, slope, True), load_shares(amount, rows * top, limit, slope, False)
    places = jnp.arange(amount)

    def named(tallies, rotation):
        used = int((tallies > 0).sum())
        fixed = max(1, used // 4)
        passed = fixed + (places - fixed + rotation * (used - fixed)) % max(1, amount - fixed)
        return jnp.zeros((amount,), jnp.int32).at[ranking[jnp.where(places < fixed, places, passed)]].set(jnp.asarray(tallies, jnp.int32))

    tallies = jnp.where(number % 4 == 0, named(crowded, number // 4), named(ordinary, number - number // 4 - 1))
    mixed = jax.random.permutation(jax.random.fold_in(own, 3), amount)
    giver, sink = mixed[0:amount // 2 * 2:2], mixed[1:amount // 2 * 2:2]
    slack = jnp.minimum(tallies[giver] - 1, limit - tallies[sink]) // 2
    slack = jnp.where((giver == ranking[0]) | (sink == ranking[0]) | (tallies[sink] == 0), 0, jnp.maximum(slack, 0))
    passed = jax.random.randint(jax.random.fold_in(own, 4), (amount // 2,), 0, 1 << 20) % (slack + 1)
    tallies = tallies.at[giver].add(-passed).at[sink].add(passed)
    members = jnp.searchsorted(jnp.cumsum(tallies), jnp.arange(rows * top), side="right").astype(jnp.int32)
    listing = members.reshape(top, rows).T
    listing = listing[jax.random.permutation(jax.random.fold_in(own, 1), rows)]
    rotation = jax.random.randint(jax.random.fold_in(own, 2), (rows, 1), 0, top)
    return jnp.take_along_axis(listing, (jnp.arange(top)[None, :] + rotation) % top, axis=1)


def load_shares(count, total, most, lean, full):
    weights = [(1 << 20) // math.isqrt(rank ** lean) + 1 for rank in range(1, count + 1)]
    largest = most if full else min(most, max(-(-total // count), total * weights[0] // sum(weights)))
    least = 1 if total - largest >= count - 1 else 0
    given, spare = [largest] + [least] * (count - 1), total - largest - least * (count - 1)
    while spare > 0:
        free = [i for i in range(1, count) if given[i] < largest] or [i for i in range(1, count) if given[i] < most]
        mass, budget = sum([weights[i] for i in free]), spare
        for i in free:
            extra = min(most - given[i], max(1, budget * weights[i] // mass), spare)
            given[i] = given[i] + extra
            spare = spare - extra
    return np.array(given)


def noise(key, shape, scale, bound, split=(), held_as=jnp.bfloat16):
    result = scale * jax.random.normal(key, shape, jnp.float32)
    if split:
        result = result * block_scale(key, shape, split, -0.22, 0.18)
    return jnp.clip(result, -bound, bound).astype(held_as)


def setup_inputs(seed: int = 0, part: int = 0) -> dict:
    key_list = jax.random.split(jax.random.key(seed), 11)
    part_splits = jax.random.split(jax.random.fold_in(key_list[10], part), 11)
    queries = draw_queries(jax.random.fold_in(jax.random.fold_in(key_list[10], part), 71), part)
    keys = draw_keys(jax.random.fold_in(jax.random.fold_in(key_list[10], part), 71), part)
    values = noise(part_splits[2], (LENGTH, D), 2.0, 12.0, ((0, 4), (1, 4)))
    tokens = draw_tokens(jax.random.fold_in(jax.random.fold_in(key_list[10], part), 71), part)
    modulation = noise(part_splits[4], (3, D), 0.5, 3.0, (), jnp.float32)
    out_weight = noise(key_list[5], (D, D), (D // 4) ** -0.5, 0.21875, ((0, 4),))
    fc_in = noise(key_list[6], (EXPERTS, H, D), D ** -0.5, 0.109375, ((0, 8), (1, 2)))
    fc_out = noise(key_list[7], (EXPERTS, H, D), H ** -0.5, 0.15625, ((0, 8), (1, 2)))
    expert_ids_keys = jax.random.split(jax.random.fold_in(part_splits[8], 1), LENGTH // TOK_DEV)
    expert_ids_turns = jax.random.permutation(jax.random.fold_in(part_splits[8], 3), LENGTH // TOK_DEV)
    expert_ids = jax.vmap(lambda own, number: deal_out(jax.random.fold_in(part_splits[8], 2), own, number, TOK_DEV, EXPERTS, TOP, CAP, 1))(expert_ids_keys, expert_ids_turns).reshape((LENGTH, TOP))
    gate_weights = jnp.clip(0.1 + 0.9 * jax.random.uniform(part_splits[9], (LENGTH, TOP), jnp.float32) ** block_scale(part_splits[9], (LENGTH, TOP), ((0, 16),), -0.2, 0.2), 0.1, 1.0)
    return {"queries": queries, "keys": keys, "values": values, "tokens": tokens, "modulation": modulation, "out_weight": out_weight, "fc_in": fc_in, "fc_out": fc_out, "expert_ids": expert_ids, "gate_weights": gate_weights}


def head_attention(operands):
    query_head, key_head, value_head = operands
    scores = jnp.dot(query_head, key_head.T, preferred_element_type=jnp.float32) / math.sqrt(HEAD_DIM)
    top_score = lax.optimization_barrier(jnp.max(scores, axis=1, keepdims=True))
    exp_scores = jnp.exp(scores - top_score)
    row_total = lax.optimization_barrier(jnp.sum(exp_scores, axis=1, keepdims=True))
    mixed = jnp.dot(exp_scores.astype(jnp.bfloat16), value_head, preferred_element_type=jnp.float32)
    return (mixed / row_total).astype(jnp.bfloat16)

def expert_apply(operands):
    slot_rows, weight_in, weight_out = operands
    hidden_act = jax.nn.gelu(jnp.dot(slot_rows, weight_in.T, preferred_element_type=jnp.float32), approximate=True)
    hidden_act = hidden_act.astype(jnp.bfloat16)
    return jnp.dot(hidden_act, weight_out, preferred_element_type=jnp.float32).astype(jnp.bfloat16)

def reference(queries, keys, values, tokens, modulation, out_weight, fc_in, fc_out, expert_ids, gate_weights):
    query_heads = queries.reshape(LENGTH, HEADS, HEAD_DIM).transpose(1, 0, 2)
    key_heads = keys.reshape(LENGTH, HEADS, HEAD_DIM).transpose(1, 0, 2)
    value_heads = values.reshape(LENGTH, HEADS, HEAD_DIM).transpose(1, 0, 2)
    attended = lax.map(head_attention, (query_heads, key_heads, value_heads))
    attended = attended.transpose(1, 0, 2).reshape(LENGTH, D)
    projected = jnp.dot(attended, out_weight, preferred_element_type=jnp.float32)
    residual = (tokens.astype(jnp.float32) + projected).astype(jnp.bfloat16)
    resid_full = residual.astype(jnp.float32)
    center = lax.optimization_barrier(jnp.mean(resid_full, axis=1, keepdims=True))
    spread = lax.optimization_barrier(jnp.mean((resid_full - center) ** 2, axis=1, keepdims=True))
    normed = (resid_full - center) * lax.rsqrt(spread + 1e-06) * (1.0 + modulation[1]) + modulation[0]
    normed = normed.astype(jnp.bfloat16)
    flat_ids = expert_ids.reshape(-1).astype(jnp.int32)
    onehot_ids = (flat_ids[:, None] == jnp.arange(EXPERTS, dtype=jnp.int32)[None, :]).astype(jnp.int32)
    earlier = jnp.cumsum(onehot_ids, axis=0) - onehot_ids
    slot_ids = lax.optimization_barrier(jnp.sum(earlier * onehot_ids, axis=1)).astype(jnp.int32)
    bucket = LENGTH // TOK_DEV * CAP
    target = (flat_ids * bucket + slot_ids).astype(jnp.int32)
    repeated = jnp.repeat(normed, TOP, axis=0)
    buffer_rows = jnp.zeros((EXPERTS * bucket, D), jnp.bfloat16).at[target].set(repeated)
    buffer_rows = buffer_rows.reshape(EXPERTS, bucket, D)
    results = lax.map(expert_apply, (buffer_rows, fc_in, fc_out)).reshape(EXPERTS * bucket, D)
    picked = results[target].astype(jnp.float32).reshape(LENGTH, TOP, D)
    mixture = lax.optimization_barrier(jnp.sum(picked * gate_weights[:, :, None].astype(jnp.float32), axis=1))
    return (resid_full + modulation[2] * mixture).astype(jnp.bfloat16)
```

```python
import math
from functools import partial

import jax
import jax.numpy as jnp
from jax import lax
from jax.experimental import pallas as pl
from jax.experimental.pallas import tpu as pltpu
from jax.sharding import PartitionSpec as P

HEAD_DIM = 128
TOP = 2
EPSILON = 1e-06
LOG2E = 1.4426950408889634
VMEM_LIMIT = 60 * 1024 * 1024


def expert_block(slot_rows, weight_in, weight_out):
    hidden_act = jax.nn.gelu(
        jnp.einsum("sd,hd->sh", slot_rows, weight_in, preferred_element_type=jnp.float32),
        approximate=True,
    )
    return jnp.dot(hidden_act.astype(jnp.bfloat16), weight_out, preferred_element_type=jnp.float32)


def attend_tile(query, key_list, value_list):
    factor = LOG2E / math.sqrt(HEAD_DIM)
    scores = [
        lax.dot_general(query, k, (((1,), (1,)), ((), ())), preferred_element_type=jnp.float32)
        for k in key_list
    ]
    top = scores[0].max(axis=1, keepdims=True)
    for s in scores[1:]:
        top = jnp.maximum(top, s.max(axis=1, keepdims=True))
    total, mixed = 0.0, 0.0
    for s, v in zip(scores, value_list):
        p = jnp.exp2((s - top) * factor)
        total = total + p.sum(axis=1, keepdims=True)
        mixed = mixed + jnp.dot(p.astype(jnp.bfloat16), v, preferred_element_type=jnp.float32)
    return (mixed / total).astype(jnp.bfloat16)


def attention_kernel(parts, query_ref, *refs):
    out_ref = refs[-1]
    keys = [refs[2 * i][...].reshape(-1, HEAD_DIM) for i in range(parts)]
    values = [refs[2 * i + 1][...].reshape(-1, HEAD_DIM) for i in range(parts)]
    out_ref[...] = attend_tile(query_ref[0, 0], keys, values)


def attention(packs, tile):
    planes, _, rows, _ = packs[0].shape
    per = rows // tile
    specs = [pl.BlockSpec((1, 1, tile, HEAD_DIM), lambda i: (i // per, 0, i % per, 0))]
    operands = [packs[0]]
    for pack in packs:
        for which in (1, 2):
            specs.append(
                pl.BlockSpec(
                    (planes, 1, pack.shape[2], HEAD_DIM), lambda i, which=which: (0, which, 0, 0)
                )
            )
            operands.append(pack)
    all_keys = sum(p.shape[0] * p.shape[2] for p in packs)
    return pl.pallas_call(
        partial(attention_kernel, len(packs)),
        grid=(planes * per,),
        in_specs=specs,
        out_specs=pl.BlockSpec((tile, HEAD_DIM), lambda i: (i, 0)),
        out_shape=jax.ShapeDtypeStruct((planes * rows, HEAD_DIM), jnp.bfloat16),
        compiler_params=pltpu.CompilerParams(vmem_limit_bytes=VMEM_LIMIT),
        cost_estimate=pl.CostEstimate(
            flops=4 * planes * rows * all_keys * HEAD_DIM,
            transcendentals=planes * rows * all_keys,
            bytes_accessed=2 * HEAD_DIM * (2 * planes * rows + 2 * all_keys),
        ),
        name="attention",
    )(*operands)


def swap(axis):
    return partial(lax.ppermute, axis_name=axis, perm=[(0, 1), (1, 0)])


def project_kernel(counts, slots_ref, full_ref, shared_ref, tokens_ref, mod_ref, *refs):
    pieces = refs[: len(counts)]
    residual_ref, normed_ref, buf, acc, sems = refs[len(counts) :]
    copies, slot = [], 0
    for piece, count in zip(pieces, counts):
        for i in range(count):
            copies.append(
                pltpu.make_async_copy(
                    piece.at[pl.ds(i * HEAD_DIM, HEAD_DIM), :],
                    buf.at[pl.ds(slot * HEAD_DIM, HEAD_DIM), :],
                    sems.at[slot],
                )
            )
            slot += 1
    for copy in copies:
        copy.start()
    full_heads = full_ref.shape[0]

    def head(i):
        where = slots_ref[i]
        is_full = where < full_heads
        one = full_ref[jnp.minimum(where, full_heads - 1)]
        two = shared_ref[jnp.maximum(where - full_heads, 0)]
        return jnp.where(is_full, one, two)

    acc[...] = tokens_ref[...].astype(jnp.float32)
    for i in range(0, slot, 2):
        copies[i].wait()
        copies[i + 1].wait()
        left = jnp.concatenate([head(i), head(i + 1)], axis=1)
        acc[...] += jnp.dot(
            left, buf[pl.ds(i * HEAD_DIM, 2 * HEAD_DIM), :], preferred_element_type=jnp.float32
        )
    residual = acc[...].astype(jnp.bfloat16)
    residual_ref[...] = residual
    full = residual.astype(jnp.float32)
    center = jnp.mean(full, axis=1, keepdims=True)
    spread = jnp.mean((full - center) ** 2, axis=1, keepdims=True)
    normed = (full - center) * lax.rsqrt(spread + EPSILON) * (1.0 + mod_ref[1:2, :]) + mod_ref[0:1, :]
    normed_ref[...] = normed.astype(jnp.bfloat16)


def moved_heads_attention(queries, keys, values, tokens, modulation, out_weight):
    planes = lax.axis_size("seq")
    query_rows, features = queries.shape
    heads = features // HEAD_DIM
    blocks = lax.axis_size(("expert", "fsdp"))
    token_rows = tokens.shape[0]
    half = token_rows // 2
    mine = [t.reshape(query_rows, heads, HEAD_DIM) for t in (queries, keys, values)]

    first = jnp.stack([t[:, :planes].transpose(1, 0, 2) for t in mine], axis=1)
    other = jnp.stack(
        [
            t[:, planes:].reshape(blocks, 2, half, heads - planes, HEAD_DIM).transpose(1, 3, 0, 2, 4)
            for t in mine
        ],
        axis=2,
    ).reshape(2, heads - planes, 3, blocks * half, HEAD_DIM)
    first_in = lax.all_to_all(first, "seq", split_axis=0, concat_axis=0, tiled=True)
    core = lax.axis_index("fsdp")
    sent = lax.dynamic_index_in_dim(other, 1 - core, 0, keepdims=False)
    kept = lax.dynamic_index_in_dim(other, core, 0, keepdims=False)
    came = swap("fsdp")(sent)
    second = jnp.where(
        core == 0, jnp.concatenate([kept, came], 0), jnp.concatenate([came, kept], 0)
    )
    second_in = lax.all_to_all(second, "seq", split_axis=0, concat_axis=0, tiled=True)
    second_pair = swap("fsdp")(second_in)

    group = lax.axis_index("group")
    rows_half = (heads // 2) * HEAD_DIM
    to_x = lax.dynamic_slice_in_dim(out_weight, group * rows_half, rows_half, 0)
    pieces = [out_weight, swap("fsdp")(out_weight)]
    from_x, from_y = [], []
    for i in range(heads // 2):
        from_x.append(swap("expert")(to_x[i * HEAD_DIM : (i + 1) * HEAD_DIM]))
    for piece in from_x:
        from_y.append(swap("group")(piece))
    pieces += from_x + from_y
    pieces += [swap("fsdp")(p) for p in from_x + from_y]

    tile = min(256, query_rows)
    first_out = attention([first_in], tile)
    first_back = lax.all_to_all(
        first_out.reshape(planes * blocks, token_rows, HEAD_DIM),
        ("seq", "expert", "fsdp"),
        split_axis=0,
        concat_axis=0,
        tiled=True,
    )
    second_out = attention([second_in, second_pair], tile)
    second_back = lax.all_to_all(
        second_out.reshape(planes * blocks, half, HEAD_DIM),
        ("seq", "expert", "fsdp"),
        split_axis=0,
        concat_axis=0,
        tiled=True,
    ).reshape(planes * 2, token_rows, HEAD_DIM)

    col = lax.axis_index("expert")
    full_heads = planes * blocks

    def slots(x, c, which):
        return [
            p * blocks + 2 * x + c
            if p < planes
            else full_heads + (2 * c + p - planes) * 2 + x
            for p in which
        ]

    everything = jnp.arange(heads)

    def slot_of(x, c, p):
        return jnp.where(
            p < planes, p * blocks + 2 * x + c, full_heads + (2 * c + p - planes) * 2 + x
        )

    near = group * (heads // 2) + jnp.arange(heads // 2)
    far = (1 - group) * (heads // 2) + jnp.arange(heads // 2)
    table = jnp.concatenate(
        [
            slot_of(col, core, everything),
            slot_of(col, 1 - core, everything),
            slot_of(1 - col, core, near),
            slot_of(1 - col, core, far),
            slot_of(1 - col, 1 - core, near),
            slot_of(1 - col, 1 - core, far),
        ]
    ).astype(jnp.int32)
    counts = tuple(p.shape[0] // HEAD_DIM for p in pieces)
    width = out_weight.shape[1]
    total = sum(counts)
    vmem = pl.BlockSpec(memory_space=pltpu.VMEM)
    return pl.pallas_call(
        partial(project_kernel, counts),
        in_specs=[pl.BlockSpec(memory_space=pltpu.SMEM)]
        + [vmem] * 4
        + [pl.BlockSpec(memory_space=pl.ANY)] * len(pieces),
        out_specs=[vmem, vmem],
        out_shape=[jax.ShapeDtypeStruct((token_rows, width), jnp.bfloat16)] * 2,
        scratch_shapes=[
            pltpu.VMEM((total * HEAD_DIM, width), jnp.bfloat16),
            pltpu.VMEM((token_rows, width), jnp.float32),
            pltpu.SemaphoreType.DMA((total,)),
        ],
        compiler_params=pltpu.CompilerParams(vmem_limit_bytes=VMEM_LIMIT),
        cost_estimate=pl.CostEstimate(
            flops=2 * token_rows * total * HEAD_DIM * width,
            transcendentals=0,
            bytes_accessed=2 * total * HEAD_DIM * width,
        ),
        name="project",
    )(table, first_back, second_back, tokens, modulation, *pieces)


def gathered_attention(queries, keys, values, tokens, modulation, out_weight):
    query_rows, features = queries.shape
    head_count = features // HEAD_DIM
    query_heads = queries.reshape(query_rows, head_count, HEAD_DIM)
    key_piece = lax.all_gather(keys, "seq", axis=0, tiled=True)
    value_piece = lax.all_gather(values, "seq", axis=0, tiled=True)
    piece_rows = key_piece.shape[0]
    key_heads = key_piece.reshape(piece_rows, head_count, HEAD_DIM)
    value_heads = value_piece.reshape(piece_rows, head_count, HEAD_DIM)
    scores = jnp.einsum(
        "qhd,khd->qhk", query_heads, key_heads, preferred_element_type=jnp.float32
    ) * (1.0 / math.sqrt(HEAD_DIM))
    exp_scores = jnp.exp(scores - jnp.max(scores, axis=-1, keepdims=True))
    weighted = jnp.einsum(
        "qhk,khd->qhd",
        exp_scores.astype(jnp.bfloat16),
        value_heads,
        preferred_element_type=jnp.float32,
    )
    attended = weighted / jnp.sum(exp_scores, axis=-1)[:, :, None]
    attended = attended.reshape(query_rows, features).astype(jnp.bfloat16)
    projected = lax.psum_scatter(
        jnp.dot(attended, out_weight, preferred_element_type=jnp.float32).astype(jnp.bfloat16),
        ("expert", "fsdp"),
        scatter_dimension=0,
        tiled=True,
    ).astype(jnp.float32)
    residual = (tokens.astype(jnp.float32) + projected).astype(jnp.bfloat16)
    resid_full = residual.astype(jnp.float32)
    center = jnp.mean(resid_full, axis=1, keepdims=True)
    spread = jnp.mean((resid_full - center) ** 2, axis=1, keepdims=True)
    normed = (resid_full - center) * lax.rsqrt(spread + EPSILON) * (
        1.0 + modulation[1]
    ) + modulation[0]
    return residual, normed.astype(jnp.bfloat16)


def sent_tokens_experts(normed, fc_in, fc_out, expert_ids, gate_weights):
    token_rows, width = normed.shape
    experts_total = fc_in.shape[0] * lax.axis_size(("seq", "expert"))
    capacity = max(2, 2 * TOP * token_rows // experts_total)
    flat_ids = expert_ids.reshape(-1)
    onehot_ids = (flat_ids[:, None] == jnp.arange(experts_total, dtype=jnp.int32)[None, :]).astype(
        jnp.int32
    )
    earlier = jnp.cumsum(onehot_ids, axis=0) - onehot_ids
    slot_ids = jnp.sum(earlier * onehot_ids, axis=1)
    target = flat_ids * capacity + slot_ids
    repeated = jnp.repeat(normed, TOP, axis=0)
    outgoing = jnp.zeros((experts_total * capacity, width), jnp.bfloat16).at[target].set(repeated)
    outgoing = outgoing.reshape(experts_total, capacity, width)
    incoming = lax.all_to_all(outgoing, ("seq", "expert"), split_axis=0, concat_axis=0, tiled=True)
    flat_incoming = incoming.reshape(experts_total * capacity, width)
    expert_sum = expert_block(
        flat_incoming,
        lax.all_gather(fc_in, "fsdp", axis=1, tiled=True)[0],
        lax.all_gather(fc_out, "fsdp", axis=1, tiled=True)[0],
    )
    results = expert_sum.astype(jnp.bfloat16).reshape(experts_total, capacity, width)
    returned = lax.all_to_all(
        results, ("seq", "expert"), split_axis=0, concat_axis=0, tiled=True
    ).reshape(experts_total * capacity, width)
    picked = returned[target].astype(jnp.float32).reshape(token_rows, TOP, width)
    return jnp.sum(picked * gate_weights[:, :, None], axis=1)


def per_device(
    queries, keys, values, tokens, modulation, out_weight, fc_in, fc_out, expert_ids, gate_weights
):
    planes = lax.axis_size("seq")
    heads = queries.shape[1] // HEAD_DIM
    pairs = all(lax.axis_size(a) == 2 for a in ("group", "expert", "fsdp"))
    if pairs and heads % 2 == 0 and heads > planes and 2 * (heads - planes) == planes:
        residual, normed = moved_heads_attention(
            queries, keys, values, tokens, modulation, out_weight
        )
    else:
        residual, normed = gathered_attention(
            queries, keys, values, tokens, modulation, out_weight
        )
    mixture = sent_tokens_experts(normed, fc_in, fc_out, expert_ids, gate_weights)
    return (residual.astype(jnp.float32) + modulation[2] * mixture).astype(jnp.bfloat16)


def solution(mesh):
    placed = (
        P(("group", "seq"), ("expert", "fsdp")),
        P(("group", "seq"), ("expert", "fsdp")),
        P(("group", "seq"), ("expert", "fsdp")),
        P(("group", "seq", "expert", "fsdp"), None),
        P("group", None),
        P(("expert", "fsdp"), None),
        P(("seq", "expert"), "fsdp", None),
        P(("seq", "expert"), "fsdp", None),
        P(("group", "seq", "expert", "fsdp"), None),
        P(("group", "seq", "expert", "fsdp"), None),
    )
    return jax.shard_map(
        per_device,
        mesh=mesh,
        in_specs=placed,
        out_specs=P(("group", "seq", "expert", "fsdp"), None),
        check_vma=False,
    )
```

```python
import math
from functools import partial

import jax
import jax.numpy as jnp
from jax import lax
from jax.experimental import pallas as pl
from jax.experimental.pallas import tpu as pltpu
from jax.sharding import PartitionSpec as P


HEAD_DIM = 128
TOP = 2
EPSILON = 1e-06
LOG2E = 1.4426950408889634
VMEM_LIMIT = 60 * 1024 * 1024


def expert_block(slot_rows, weight_in, weight_out):
    hidden_act = jax.nn.gelu(
        jnp.einsum("sd,hd->sh", slot_rows, weight_in, preferred_element_type=jnp.float32),
        approximate=True,
    )
    return jnp.dot(hidden_act.astype(jnp.bfloat16), weight_out, preferred_element_type=jnp.float32)


def attend_tile(query, key_list, value_list):
    factor = LOG2E / math.sqrt(HEAD_DIM)
    scores = [
        lax.dot_general(query, k, (((1,), (1,)), ((), ())), preferred_element_type=jnp.float32)
        for k in key_list
    ]
    top = scores[0].max(axis=1, keepdims=True)
    for s in scores[1:]:
        top = jnp.maximum(top, s.max(axis=1, keepdims=True))
    total, mixed = 0.0, 0.0
    for s, v in zip(scores, value_list):
        p = jnp.exp2((s - top) * factor)
        total = total + p.sum(axis=1, keepdims=True)
        mixed = mixed + jnp.dot(p.astype(jnp.bfloat16), v, preferred_element_type=jnp.float32)
    return (mixed / total).astype(jnp.bfloat16)


def attention_kernel(parts, query_ref, *refs):
    out_ref = refs[-1]
    keys = [refs[2 * i][...].reshape(-1, HEAD_DIM) for i in range(parts)]
    values = [refs[2 * i + 1][...].reshape(-1, HEAD_DIM) for i in range(parts)]
    out_ref[...] = attend_tile(query_ref[0, 0], keys, values)


def attention(packs, tile):
    planes, _, rows, _ = packs[0].shape
    per = rows // tile
    specs = [pl.BlockSpec((1, 1, tile, HEAD_DIM), lambda i: (i // per, 0, i % per, 0))]
    operands = [packs[0]]
    for pack in packs:
        for which in (1, 2):
            specs.append(
                pl.BlockSpec(
                    (planes, 1, pack.shape[2], HEAD_DIM), lambda i, which=which: (0, which, 0, 0)
                )
            )
            operands.append(pack)
    all_keys = sum(p.shape[0] * p.shape[2] for p in packs)
    return pl.pallas_call(
        partial(attention_kernel, len(packs)),
        grid=(planes * per,),
        in_specs=specs,
        out_specs=pl.BlockSpec((tile, HEAD_DIM), lambda i: (i, 0)),
        out_shape=jax.ShapeDtypeStruct((planes * rows, HEAD_DIM), jnp.bfloat16),
        compiler_params=pltpu.CompilerParams(vmem_limit_bytes=VMEM_LIMIT),
        cost_estimate=pl.CostEstimate(
            flops=4 * planes * rows * all_keys * HEAD_DIM,
            transcendentals=planes * rows * all_keys,
            bytes_accessed=2 * HEAD_DIM * (2 * planes * rows + 2 * all_keys),
        ),
        name="attention",
    )(*operands)


def pack_kernel(planes, half, core_ref, q_ref, k_ref, v_ref, first_ref, kept_ref, sent_ref):
    core = core_ref[0]
    for which, ref in enumerate((q_ref, k_ref, v_ref)):
        heads = ref.shape[1] // HEAD_DIM
        for h in range(heads):
            columns = slice(h * HEAD_DIM, (h + 1) * HEAD_DIM)
            if h < planes:
                first_ref[h, which] = ref[:, columns]
                continue
            for out, side in ((kept_ref, core), (sent_ref, 1 - core)):
                for j in range(ref.shape[0] // (2 * half)):
                    start = pl.multiple_of(j * 2 * half + side * half, half)
                    out[h - planes, which, j * half : (j + 1) * half] = ref[
                        pl.ds(start, half), columns
                    ]


def swap(axis):
    return partial(lax.ppermute, axis_name=axis, perm=[(0, 1), (1, 0)])


def project_kernel(counts, slots_ref, full_ref, shared_ref, tokens_ref, mod_ref, *refs):
    pieces = refs[: len(counts)]
    residual_ref, normed_ref, buf, acc, sems = refs[len(counts) :]
    copies, slot = [], 0
    for piece, count in zip(pieces, counts):
        for i in range(count):
            copies.append(
                pltpu.make_async_copy(
                    piece.at[pl.ds(i * HEAD_DIM, HEAD_DIM), :],
                    buf.at[pl.ds(slot * HEAD_DIM, HEAD_DIM), :],
                    sems.at[slot],
                )
            )
            slot += 1
    for copy in copies:
        copy.start()
    full_heads = full_ref.shape[0]

    def head(i):
        where = slots_ref[i]
        is_full = where < full_heads
        one = full_ref[jnp.minimum(where, full_heads - 1)]
        two = shared_ref[jnp.maximum(where - full_heads, 0)]
        return jnp.where(is_full, one, two)

    acc[...] = tokens_ref[...].astype(jnp.float32)
    for i in range(0, slot, 2):
        copies[i].wait()
        copies[i + 1].wait()
        left = jnp.concatenate([head(i), head(i + 1)], axis=1)
        acc[...] += jnp.dot(
            left, buf[pl.ds(i * HEAD_DIM, 2 * HEAD_DIM), :], preferred_element_type=jnp.float32
        )
    residual = acc[...].astype(jnp.bfloat16)
    residual_ref[...] = residual
    full = residual.astype(jnp.float32)
    center = jnp.mean(full, axis=1, keepdims=True)
    spread = jnp.mean((full - center) ** 2, axis=1, keepdims=True)
    normed = (full - center) * lax.rsqrt(spread + EPSILON) * (1.0 + mod_ref[1:2, :]) + mod_ref[0:1, :]
    normed_ref[...] = normed.astype(jnp.bfloat16)


def moved_heads_attention(queries, keys, values, tokens, modulation, out_weight):
    planes = lax.axis_size("seq")
    query_rows, features = queries.shape
    heads = features // HEAD_DIM
    blocks = lax.axis_size(("expert", "fsdp"))
    token_rows = tokens.shape[0]
    half = token_rows // 2
    core = lax.axis_index("fsdp")
    vmem = pl.BlockSpec(memory_space=pltpu.VMEM)
    own = (heads - planes, 3, blocks * half, HEAD_DIM)
    first, kept, sent = pl.pallas_call(
        partial(pack_kernel, planes, half),
        in_specs=[pl.BlockSpec(memory_space=pltpu.SMEM)] + [vmem] * 3,
        out_specs=[vmem] * 3,
        out_shape=[
            jax.ShapeDtypeStruct((planes, 3, query_rows, HEAD_DIM), jnp.bfloat16),
            jax.ShapeDtypeStruct(own, jnp.bfloat16),
            jax.ShapeDtypeStruct(own, jnp.bfloat16),
        ],
        compiler_params=pltpu.CompilerParams(vmem_limit_bytes=VMEM_LIMIT),
        name="pack",
    )(core.reshape(1), queries, keys, values)
    first_in = lax.all_to_all(first, "seq", split_axis=0, concat_axis=0, tiled=True)
    came = swap("fsdp")(sent)
    second = jnp.where(
        core == 0, jnp.concatenate([kept, came], 0), jnp.concatenate([came, kept], 0)
    )
    second_in = lax.all_to_all(second, "seq", split_axis=0, concat_axis=0, tiled=True)
    second_pair = swap("fsdp")(second_in)

    group = lax.axis_index("group")
    rows_half = (heads // 2) * HEAD_DIM
    to_x = lax.dynamic_slice_in_dim(out_weight, group * rows_half, rows_half, 0)
    pieces = [out_weight, swap("fsdp")(out_weight)]
    from_x, from_y = [], []
    for i in range(heads // 2):
        from_x.append(swap("expert")(to_x[i * HEAD_DIM : (i + 1) * HEAD_DIM]))
    for piece in from_x:
        from_y.append(swap("group")(piece))
    pieces += from_x + from_y
    pieces += [swap("fsdp")(p) for p in from_x + from_y]

    tile = min(256, query_rows)
    first_out = attention([first_in], tile)
    first_back = lax.all_to_all(
        first_out.reshape(planes * blocks, token_rows, HEAD_DIM),
        ("seq", "expert", "fsdp"),
        split_axis=0,
        concat_axis=0,
        tiled=True,
    )
    second_out = attention([second_in, second_pair], tile)
    second_back = lax.all_to_all(
        second_out.reshape(planes * blocks, half, HEAD_DIM),
        ("seq", "expert", "fsdp"),
        split_axis=0,
        concat_axis=0,
        tiled=True,
    ).reshape(planes * 2, token_rows, HEAD_DIM)

    col = lax.axis_index("expert")
    full_heads = planes * blocks

    everything = jnp.arange(heads)

    def slot_of(x, c, p):
        return jnp.where(
            p < planes, p * blocks + 2 * x + c, full_heads + (2 * c + p - planes) * 2 + x
        )

    near = group * (heads // 2) + jnp.arange(heads // 2)
    far = (1 - group) * (heads // 2) + jnp.arange(heads // 2)
    table = jnp.concatenate(
        [
            slot_of(col, core, everything),
            slot_of(col, 1 - core, everything),
            slot_of(1 - col, core, near),
            slot_of(1 - col, core, far),
            slot_of(1 - col, 1 - core, near),
            slot_of(1 - col, 1 - core, far),
        ]
    ).astype(jnp.int32)
    counts = tuple(p.shape[0] // HEAD_DIM for p in pieces)
    width = out_weight.shape[1]
    total = sum(counts)
    return pl.pallas_call(
        partial(project_kernel, counts),
        in_specs=[pl.BlockSpec(memory_space=pltpu.SMEM)]
        + [vmem] * 4
        + [pl.BlockSpec(memory_space=pl.ANY)] * len(pieces),
        out_specs=[vmem, vmem],
        out_shape=[jax.ShapeDtypeStruct((token_rows, width), jnp.bfloat16)] * 2,
        scratch_shapes=[
            pltpu.VMEM((total * HEAD_DIM, width), jnp.bfloat16),
            pltpu.VMEM((token_rows, width), jnp.float32),
            pltpu.SemaphoreType.DMA((total,)),
        ],
        compiler_params=pltpu.CompilerParams(vmem_limit_bytes=VMEM_LIMIT),
        cost_estimate=pl.CostEstimate(
            flops=2 * token_rows * total * HEAD_DIM * width,
            transcendentals=0,
            bytes_accessed=2 * total * HEAD_DIM * width,
        ),
        name="project",
    )(table, first_back, second_back, tokens, modulation, *pieces)


def gathered_attention(queries, keys, values, tokens, modulation, out_weight):
    query_rows, features = queries.shape
    head_count = features // HEAD_DIM
    query_heads = queries.reshape(query_rows, head_count, HEAD_DIM)
    key_piece = lax.all_gather(keys, "seq", axis=0, tiled=True)
    value_piece = lax.all_gather(values, "seq", axis=0, tiled=True)
    piece_rows = key_piece.shape[0]
    key_heads = key_piece.reshape(piece_rows, head_count, HEAD_DIM)
    value_heads = value_piece.reshape(piece_rows, head_count, HEAD_DIM)
    scores = jnp.einsum(
        "qhd,khd->qhk", query_heads, key_heads, preferred_element_type=jnp.float32
    ) * (1.0 / math.sqrt(HEAD_DIM))
    exp_scores = jnp.exp(scores - jnp.max(scores, axis=-1, keepdims=True))
    weighted = jnp.einsum(
        "qhk,khd->qhd",
        exp_scores.astype(jnp.bfloat16),
        value_heads,
        preferred_element_type=jnp.float32,
    )
    attended = weighted / jnp.sum(exp_scores, axis=-1)[:, :, None]
    attended = attended.reshape(query_rows, features).astype(jnp.bfloat16)
    projected = lax.psum_scatter(
        jnp.dot(attended, out_weight, preferred_element_type=jnp.float32).astype(jnp.bfloat16),
        ("expert", "fsdp"),
        scatter_dimension=0,
        tiled=True,
    ).astype(jnp.float32)
    residual = (tokens.astype(jnp.float32) + projected).astype(jnp.bfloat16)
    resid_full = residual.astype(jnp.float32)
    center = jnp.mean(resid_full, axis=1, keepdims=True)
    spread = jnp.mean((resid_full - center) ** 2, axis=1, keepdims=True)
    normed = (resid_full - center) * lax.rsqrt(spread + EPSILON) * (
        1.0 + modulation[1]
    ) + modulation[0]
    return residual, normed.astype(jnp.bfloat16)


def sent_tokens_experts(normed, fc_in, fc_out, expert_ids, gate_weights):
    token_rows, width = normed.shape
    experts_total = fc_in.shape[0] * lax.axis_size(("seq", "expert"))
    capacity = max(2, 2 * TOP * token_rows // experts_total)
    flat_ids = expert_ids.reshape(-1)
    onehot_ids = (flat_ids[:, None] == jnp.arange(experts_total, dtype=jnp.int32)[None, :]).astype(
        jnp.int32
    )
    earlier = jnp.cumsum(onehot_ids, axis=0) - onehot_ids
    slot_ids = jnp.sum(earlier * onehot_ids, axis=1)
    target = flat_ids * capacity + slot_ids
    repeated = jnp.repeat(normed, TOP, axis=0)
    outgoing = jnp.zeros((experts_total * capacity, width), jnp.bfloat16).at[target].set(repeated)
    outgoing = outgoing.reshape(experts_total, capacity, width)
    incoming = lax.all_to_all(outgoing, ("seq", "expert"), split_axis=0, concat_axis=0, tiled=True)
    flat_incoming = incoming.reshape(experts_total * capacity, width)
    expert_sum = expert_block(
        flat_incoming,
        lax.all_gather(fc_in, "fsdp", axis=1, tiled=True)[0],
        lax.all_gather(fc_out, "fsdp", axis=1, tiled=True)[0],
    )
    results = expert_sum.astype(jnp.bfloat16).reshape(experts_total, capacity, width)
    returned = lax.all_to_all(
        results, ("seq", "expert"), split_axis=0, concat_axis=0, tiled=True
    ).reshape(experts_total * capacity, width)
    picked = returned[target].astype(jnp.float32).reshape(token_rows, TOP, width)
    return jnp.sum(picked * gate_weights[:, :, None], axis=1)


def per_device(
    queries, keys, values, tokens, modulation, out_weight, fc_in, fc_out, expert_ids, gate_weights
):
    planes = lax.axis_size("seq")
    heads = queries.shape[1] // HEAD_DIM
    pairs = all(lax.axis_size(a) == 2 for a in ("group", "expert", "fsdp"))
    if pairs and heads % 2 == 0 and heads > planes and 2 * (heads - planes) == planes:
        residual, normed = moved_heads_attention(
            queries, keys, values, tokens, modulation, out_weight
        )
    else:
        residual, normed = gathered_attention(
            queries, keys, values, tokens, modulation, out_weight
        )
    mixture = sent_tokens_experts(normed, fc_in, fc_out, expert_ids, gate_weights)
    return (residual.astype(jnp.float32) + modulation[2] * mixture).astype(jnp.bfloat16)


def solution(mesh):
    placed = (
        P(("group", "seq"), ("expert", "fsdp")),
        P(("group", "seq"), ("expert", "fsdp")),
        P(("group", "seq"), ("expert", "fsdp")),
        P(("group", "seq", "expert", "fsdp"), None),
        P("group", None),
        P(("expert", "fsdp"), None),
        P(("seq", "expert"), "fsdp", None),
        P(("seq", "expert"), "fsdp", None),
        P(("group", "seq", "expert", "fsdp"), None),
        P(("group", "seq", "expert", "fsdp"), None),
    )

    return jax.shard_map(
        per_device,
        mesh=mesh,
        in_specs=placed,
        out_specs=P(("group", "seq", "expert", "fsdp"), None),
        check_vma=False,
    )
```

```python
import math
from functools import partial

import jax
import jax.numpy as jnp
from jax import lax
from jax.experimental import pallas as pl
from jax.experimental.pallas import tpu as pltpu
from jax.sharding import PartitionSpec as P


HEAD_DIM = 128
TOP = 2
EPSILON = 1e-06
LOG2E = 1.4426950408889634
VMEM_LIMIT = 60 * 1024 * 1024


def expert_block(slot_rows, weight_in, weight_out):
    hidden_act = jax.nn.gelu(
        jnp.einsum("sd,hd->sh", slot_rows, weight_in, preferred_element_type=jnp.float32),
        approximate=True,
    )
    return jnp.dot(hidden_act.astype(jnp.bfloat16), weight_out, preferred_element_type=jnp.float32)


def attend_tile(query, key_list, value_list):
    factor = LOG2E / math.sqrt(HEAD_DIM)
    scores = [
        lax.dot_general(query, k, (((1,), (1,)), ((), ())), preferred_element_type=jnp.float32)
        for k in key_list
    ]
    top = scores[0].max(axis=1, keepdims=True)
    for s in scores[1:]:
        top = jnp.maximum(top, s.max(axis=1, keepdims=True))
    total, mixed = 0.0, 0.0
    for s, v in zip(scores, value_list):
        p = jnp.exp2((s - top) * factor)
        total = total + p.sum(axis=1, keepdims=True)
        mixed = mixed + jnp.dot(p.astype(jnp.bfloat16), v, preferred_element_type=jnp.float32)
    return (mixed / total).astype(jnp.bfloat16)


def attention_kernel(parts, query_ref, *refs):
    out_ref = refs[-1]
    keys = [refs[2 * i][...].reshape(-1, HEAD_DIM) for i in range(parts)]
    values = [refs[2 * i + 1][...].reshape(-1, HEAD_DIM) for i in range(parts)]
    out_ref[...] = attend_tile(query_ref[0, 0], keys, values)


def attention(packs, tile):
    planes, _, rows, _ = packs[0].shape
    per = rows // tile
    specs = [pl.BlockSpec((1, 1, tile, HEAD_DIM), lambda i: (i // per, 0, i % per, 0))]
    operands = [packs[0]]
    for pack in packs:
        for which in (1, 2):
            specs.append(
                pl.BlockSpec(
                    (planes, 1, pack.shape[2], HEAD_DIM), lambda i, which=which: (0, which, 0, 0)
                )
            )
            operands.append(pack)
    all_keys = sum(p.shape[0] * p.shape[2] for p in packs)
    return pl.pallas_call(
        partial(attention_kernel, len(packs)),
        grid=(planes * per,),
        in_specs=specs,
        out_specs=pl.BlockSpec((tile, HEAD_DIM), lambda i: (i, 0)),
        out_shape=jax.ShapeDtypeStruct((planes * rows, HEAD_DIM), jnp.bfloat16),
        compiler_params=pltpu.CompilerParams(vmem_limit_bytes=VMEM_LIMIT),
        cost_estimate=pl.CostEstimate(
            flops=4 * planes * rows * all_keys * HEAD_DIM,
            transcendentals=planes * rows * all_keys,
            bytes_accessed=2 * HEAD_DIM * (2 * planes * rows + 2 * all_keys),
        ),
        name="attention",
    )(*operands)


def pack_kernel(planes, half, core_ref, q_ref, k_ref, v_ref, first_ref, kept_ref, sent_ref):
    core = core_ref[0]
    for which, ref in enumerate((q_ref, k_ref, v_ref)):
        heads = ref.shape[1] // HEAD_DIM
        for h in range(heads):
            columns = slice(h * HEAD_DIM, (h + 1) * HEAD_DIM)
            if h < planes:
                first_ref[h, which] = ref[:, columns]
                continue
            for out, side in ((kept_ref, core), (sent_ref, 1 - core)):
                for j in range(ref.shape[0] // (2 * half)):
                    start = pl.multiple_of(j * 2 * half + side * half, half)
                    out[h - planes, which, j * half : (j + 1) * half] = ref[
                        pl.ds(start, half), columns
                    ]


def swap(axis):
    return partial(lax.ppermute, axis_name=axis, perm=[(0, 1), (1, 0)])


def project_kernel(counts, slots_ref, full_ref, shared_ref, tokens_ref, mod_ref, *refs):
    pieces = refs[: len(counts)]
    residual_ref, normed_ref, buf, acc, sems = refs[len(counts) :]
    copies, slot = [], 0
    for piece, count in zip(pieces, counts):
        for i in range(count):
            copies.append(
                pltpu.make_async_copy(
                    piece.at[pl.ds(i * HEAD_DIM, HEAD_DIM), :],
                    buf.at[pl.ds(slot * HEAD_DIM, HEAD_DIM), :],
                    sems.at[slot],
                )
            )
            slot += 1
    for copy in copies:
        copy.start()
    full_heads = full_ref.shape[0]

    def head(i):
        where = slots_ref[i]
        is_full = where < full_heads
        one = full_ref[jnp.minimum(where, full_heads - 1)]
        two = shared_ref[jnp.maximum(where - full_heads, 0)]
        return jnp.where(is_full, one, two)

    acc[...] = tokens_ref[...].astype(jnp.float32)
    for i in range(0, slot, 2):
        copies[i].wait()
        copies[i + 1].wait()
        left = jnp.concatenate([head(i), head(i + 1)], axis=1)
        acc[...] += jnp.dot(
            left, buf[pl.ds(i * HEAD_DIM, 2 * HEAD_DIM), :], preferred_element_type=jnp.float32
        )
    residual = acc[...].astype(jnp.bfloat16)
    residual_ref[...] = residual
    full = residual.astype(jnp.float32)
    center = jnp.mean(full, axis=1, keepdims=True)
    spread = jnp.mean((full - center) ** 2, axis=1, keepdims=True)
    normed = (full - center) * lax.rsqrt(spread + EPSILON) * (1.0 + mod_ref[1:2, :]) + mod_ref[0:1, :]
    normed_ref[...] = normed.astype(jnp.bfloat16)


def moved_heads_attention(queries, keys, values, tokens, modulation, out_weight):
    planes = lax.axis_size("seq")
    query_rows, features = queries.shape
    heads = features // HEAD_DIM
    blocks = lax.axis_size(("expert", "fsdp"))
    token_rows = tokens.shape[0]
    half = token_rows // 2
    core = lax.axis_index("fsdp")
    vmem = pl.BlockSpec(memory_space=pltpu.VMEM)
    own = (heads - planes, 3, blocks * half, HEAD_DIM)
    first, kept, sent = pl.pallas_call(
        partial(pack_kernel, planes, half),
        in_specs=[pl.BlockSpec(memory_space=pltpu.SMEM)] + [vmem] * 3,
        out_specs=[vmem] * 3,
        out_shape=[
            jax.ShapeDtypeStruct((planes, 3, query_rows, HEAD_DIM), jnp.bfloat16),
            jax.ShapeDtypeStruct(own, jnp.bfloat16),
            jax.ShapeDtypeStruct(own, jnp.bfloat16),
        ],
        compiler_params=pltpu.CompilerParams(vmem_limit_bytes=VMEM_LIMIT),
        name="pack",
    )(core.reshape(1), queries, keys, values)
    first_in = lax.all_to_all(first, "seq", split_axis=0, concat_axis=0, tiled=True)
    came = swap("fsdp")(sent)
    second = jnp.where(
        core == 0, jnp.concatenate([kept, came], 0), jnp.concatenate([came, kept], 0)
    )
    second_in = lax.all_to_all(second, "seq", split_axis=0, concat_axis=0, tiled=True)
    second_pair = swap("fsdp")(second_in)

    group = lax.axis_index("group")
    rows_half = (heads // 2) * HEAD_DIM
    to_x = lax.dynamic_slice_in_dim(out_weight, group * rows_half, rows_half, 0)
    pieces = [out_weight, swap("fsdp")(out_weight)]
    from_x, from_y = [], []
    for i in range(heads // 2):
        from_x.append(swap("expert")(to_x[i * HEAD_DIM : (i + 1) * HEAD_DIM]))
    for piece in from_x:
        from_y.append(swap("group")(piece))
    pieces += from_x + from_y
    pieces += [swap("fsdp")(p) for p in from_x + from_y]

    tile = min(256, query_rows)
    first_out = attention([first_in], tile)
    first_back = lax.all_to_all(
        first_out.reshape(planes * blocks, token_rows, HEAD_DIM),
        ("seq", "expert", "fsdp"),
        split_axis=0,
        concat_axis=0,
        tiled=True,
    )
    second_out = attention([second_in, second_pair], tile)
    second_back = lax.all_to_all(
        second_out.reshape(planes * blocks, half, HEAD_DIM),
        ("seq", "expert", "fsdp"),
        split_axis=0,
        concat_axis=0,
        tiled=True,
    ).reshape(planes * 2, token_rows, HEAD_DIM)

    col = lax.axis_index("expert")
    full_heads = planes * blocks

    everything = jnp.arange(heads)

    def slot_of(x, c, p):
        return jnp.where(
            p < planes, p * blocks + 2 * x + c, full_heads + (2 * c + p - planes) * 2 + x
        )

    near = group * (heads // 2) + jnp.arange(heads // 2)
    far = (1 - group) * (heads // 2) + jnp.arange(heads // 2)
    table = jnp.concatenate(
        [
            slot_of(col, core, everything),
            slot_of(col, 1 - core, everything),
            slot_of(1 - col, core, near),
            slot_of(1 - col, core, far),
            slot_of(1 - col, 1 - core, near),
            slot_of(1 - col, 1 - core, far),
        ]
    ).astype(jnp.int32)
    counts = tuple(p.shape[0] // HEAD_DIM for p in pieces)
    width = out_weight.shape[1]
    total = sum(counts)
    return pl.pallas_call(
        partial(project_kernel, counts),
        in_specs=[pl.BlockSpec(memory_space=pltpu.SMEM)]
        + [vmem] * 4
        + [pl.BlockSpec(memory_space=pl.ANY)] * len(pieces),
        out_specs=[vmem, vmem],
        out_shape=[jax.ShapeDtypeStruct((token_rows, width), jnp.bfloat16)] * 2,
        scratch_shapes=[
            pltpu.VMEM((total * HEAD_DIM, width), jnp.bfloat16),
            pltpu.VMEM((token_rows, width), jnp.float32),
            pltpu.SemaphoreType.DMA((total,)),
        ],
        compiler_params=pltpu.CompilerParams(vmem_limit_bytes=VMEM_LIMIT),
        cost_estimate=pl.CostEstimate(
            flops=2 * token_rows * total * HEAD_DIM * width,
            transcendentals=0,
            bytes_accessed=2 * total * HEAD_DIM * width,
        ),
        name="project",
    )(table, first_back, second_back, tokens, modulation, *pieces)


def gathered_attention(queries, keys, values, tokens, modulation, out_weight):
    query_rows, features = queries.shape
    head_count = features // HEAD_DIM
    query_heads = queries.reshape(query_rows, head_count, HEAD_DIM)
    key_piece = lax.all_gather(keys, "seq", axis=0, tiled=True)
    value_piece = lax.all_gather(values, "seq", axis=0, tiled=True)
    piece_rows = key_piece.shape[0]
    key_heads = key_piece.reshape(piece_rows, head_count, HEAD_DIM)
    value_heads = value_piece.reshape(piece_rows, head_count, HEAD_DIM)
    scores = jnp.einsum(
        "qhd,khd->qhk", query_heads, key_heads, preferred_element_type=jnp.float32
    ) * (1.0 / math.sqrt(HEAD_DIM))
    exp_scores = jnp.exp(scores - jnp.max(scores, axis=-1, keepdims=True))
    weighted = jnp.einsum(
        "qhk,khd->qhd",
        exp_scores.astype(jnp.bfloat16),
        value_heads,
        preferred_element_type=jnp.float32,
    )
    attended = weighted / jnp.sum(exp_scores, axis=-1)[:, :, None]
    attended = attended.reshape(query_rows, features).astype(jnp.bfloat16)
    projected = lax.psum_scatter(
        jnp.dot(attended, out_weight, preferred_element_type=jnp.float32).astype(jnp.bfloat16),
        ("expert", "fsdp"),
        scatter_dimension=0,
        tiled=True,
    ).astype(jnp.float32)
    residual = (tokens.astype(jnp.float32) + projected).astype(jnp.bfloat16)
    resid_full = residual.astype(jnp.float32)
    center = jnp.mean(resid_full, axis=1, keepdims=True)
    spread = jnp.mean((resid_full - center) ** 2, axis=1, keepdims=True)
    normed = (resid_full - center) * lax.rsqrt(spread + EPSILON) * (
        1.0 + modulation[1]
    ) + modulation[0]
    return residual, normed.astype(jnp.bfloat16)


def sent_tokens_experts(normed, fc_in, fc_out, expert_ids, gate_weights):
    token_rows, width = normed.shape
    experts_total = fc_in.shape[0] * lax.axis_size(("seq", "expert"))
    capacity = max(2, 2 * TOP * token_rows // experts_total)
    flat_ids = expert_ids.reshape(-1)
    onehot_ids = (flat_ids[:, None] == jnp.arange(experts_total, dtype=jnp.int32)[None, :]).astype(
        jnp.int32
    )
    earlier = jnp.cumsum(onehot_ids, axis=0) - onehot_ids
    slot_ids = jnp.sum(earlier * onehot_ids, axis=1)
    target = flat_ids * capacity + slot_ids
    repeated = jnp.repeat(normed, TOP, axis=0)
    outgoing = jnp.zeros((experts_total * capacity, width), jnp.bfloat16).at[target].set(repeated)
    outgoing = outgoing.reshape(experts_total, capacity, width)
    incoming = lax.all_to_all(outgoing, ("seq", "expert"), split_axis=0, concat_axis=0, tiled=True)
    flat_incoming = incoming.reshape(experts_total * capacity, width)
    expert_sum = expert_block(
        flat_incoming,
        lax.all_gather(fc_in, "fsdp", axis=1, tiled=True)[0],
        lax.all_gather(fc_out, "fsdp", axis=1, tiled=True)[0],
    )
    results = expert_sum.astype(jnp.bfloat16).reshape(experts_total, capacity, width)
    returned = lax.all_to_all(
        results, ("seq", "expert"), split_axis=0, concat_axis=0, tiled=True
    ).reshape(experts_total * capacity, width)
    picked = returned[target].astype(jnp.float32).reshape(token_rows, TOP, width)
    return jnp.sum(picked * gate_weights[:, :, None], axis=1)


def route_kernel(capacity, marks_ref, info_ref, pick_ref, gate_ref):
    planes, _, rows = info_ref.shape
    row = lax.broadcasted_iota(jnp.int32, (rows, rows), 0)
    col = lax.broadcasted_iota(jnp.int32, (rows, rows), 1)
    before = (row < col).astype(jnp.bfloat16)
    slot = lax.broadcasted_iota(jnp.int32, (capacity, rows), 0).astype(jnp.float32)
    for block in range(planes):
        for side in range(2):
            mark = marks_ref[side].astype(jnp.float32)
            named, gate = jnp.zeros((1, rows), jnp.float32), jnp.zeros((1, rows), jnp.float32)
            for k in range(TOP):
                hit = (info_ref[block, k : k + 1, :] == mark).astype(jnp.float32)
                named = named + hit
                gate = gate + hit * info_ref[block, TOP + k : TOP + k + 1, :]
            wide = jnp.broadcast_to(named, (8, rows)).astype(jnp.bfloat16)
            rank = jnp.dot(wide, before, preferred_element_type=jnp.float32)[0:1]
            pick = jnp.where((slot == rank) & (named > 0.5), 1.0, 0.0)
            pick_ref[block, side] = pick.astype(jnp.bfloat16)
            gate_ref[block, :, side : side + 1] = jnp.sum(
                jnp.where(row == col, gate, 0.0), axis=1, keepdims=True
            )


def compact_kernel(where_ref, pick_ref, *refs):
    near_ref, far_ref = refs[-2:]
    block = refs[0][...]
    if len(refs) == 4:
        block = jnp.where(where_ref[1] == 1, block, refs[1][...])
    for side, out in enumerate((near_ref, far_ref)):
        out[...] = jnp.dot(
            pick_ref[where_ref[0], side], block, preferred_element_type=jnp.float32
        ).astype(jnp.bfloat16)


def expert_kernel(near_ref, far_ref, in_ref, out_ref, near_out, far_out, acc):
    step = pl.program_id(0)
    rows = jnp.concatenate([near_ref[...], far_ref[...]], axis=0)
    pre = lax.dot_general(
        rows, in_ref[...], (((1,), (1,)), ((), ())), preferred_element_type=jnp.float32
    )
    act = jax.nn.gelu(pre, approximate=True).astype(jnp.bfloat16)
    part = jnp.dot(act, out_ref[...], preferred_element_type=jnp.float32)

    @pl.when(step == 0)
    def _():
        acc[...] = part

    @pl.when(step > 0)
    def _():
        acc[...] += part

    @pl.when(step == pl.num_programs(0) - 1)
    def _():
        half = near_out.shape[0]
        near_out[...] = acc[:half].astype(jnp.bfloat16)
        far_out[...] = acc[half:].astype(jnp.bfloat16)


def mixed_rows(block, pick_ref, gate_ref, outs):
    total = 0.0
    for side, out in enumerate(outs):
        rows = lax.dot_general(
            pick_ref[block, side],
            out[...],
            (((0,), (0,)), ((), ())),
            preferred_element_type=jnp.float32,
        )
        total = total + gate_ref[block][:, side : side + 1] * rows
    return total


def combine_kernel(where_ref, pick_ref, gate_ref, near_ref, far_ref, out_ref):
    out_ref[...] = mixed_rows(where_ref[0], pick_ref, gate_ref, (near_ref, far_ref)).astype(
        jnp.bfloat16
    )


def final_kernel(
    where_ref, pick_ref, gate_ref, near_ref, far_ref, residual_ref, mod_ref, *refs
):
    total = mixed_rows(where_ref[0], pick_ref, gate_ref, (near_ref, far_ref))
    for ref in refs[:-1]:
        total = total + ref[...].astype(jnp.float32)
    refs[-1][...] = (residual_ref[...].astype(jnp.float32) + mod_ref[2:3, :] * total).astype(
        jnp.bfloat16
    )


def small_call(kernel, shapes, flops, operands, scalars=1):
    vmem = pl.BlockSpec(memory_space=pltpu.VMEM)
    moved = sum(math.prod(o.shape) * o.dtype.itemsize for o in operands)
    return pl.pallas_call(
        kernel,
        in_specs=[pl.BlockSpec(memory_space=pltpu.SMEM)] * scalars
        + [vmem] * (len(operands) - scalars),
        out_specs=[vmem] * len(shapes),
        out_shape=shapes,
        compiler_params=pltpu.CompilerParams(vmem_limit_bytes=VMEM_LIMIT),
        cost_estimate=pl.CostEstimate(flops=flops, transcendentals=0, bytes_accessed=moved),
    )(*operands)


def passed_tokens_experts(
    residual, normed, modulation, fc_in, fc_out, expert_ids, gate_weights
):
    planes, sides = lax.axis_size("seq"), lax.axis_size("expert")
    plane, col = lax.axis_index("seq"), lax.axis_index("expert")
    token_rows, width = normed.shape
    capacity = 2 * TOP * token_rows // (planes * sides)
    info = jnp.concatenate([expert_ids.T.astype(jnp.float32), gate_weights.T], axis=0)
    info = lax.all_gather(info, "seq", axis=0, tiled=False)
    marks = jnp.stack([plane * sides + col, plane * sides + 1 - col]).astype(jnp.int32)
    pick, gate = small_call(
        partial(route_kernel, capacity),
        [
            jax.ShapeDtypeStruct((planes, 2, capacity, token_rows), jnp.bfloat16),
            jax.ShapeDtypeStruct((planes, token_rows, 2), jnp.float32),
        ],
        0,
        (marks, info),
    )
    whole_in = lax.all_gather(fc_in, "fsdp", axis=1, tiled=True)[0]
    whole_out = lax.all_gather(fc_out, "fsdp", axis=1, tiled=True)[0]
    hidden = whole_in.shape[0]
    chunk = min(256, hidden)
    slots = jax.ShapeDtypeStruct((capacity, width), jnp.bfloat16)

    def along(value, perm):
        return lax.ppermute(value, "seq", perm)

    def across(value, on):
        perm = [(p * sides + x, p * sides + 1 - x) for p in on for x in range(sides)]
        return lax.ppermute(value, ("seq", "expert"), perm)

    def compact(where, blocks):
        return small_call(
            compact_kernel,
            [slots, slots],
            4 * capacity * token_rows * width,
            (where, pick, *blocks),
        )

    def experts(near, far):
        rows = pl.BlockSpec((capacity, width), lambda i: (0, 0))
        weights = pl.BlockSpec((chunk, width), lambda i: (i, 0))
        return pl.pallas_call(
            expert_kernel,
            grid=(hidden // chunk,),
            in_specs=[rows, rows, weights, weights],
            out_specs=[rows, rows],
            out_shape=[slots, slots],
            scratch_shapes=[pltpu.VMEM((2 * capacity, width), jnp.float32)],
            compiler_params=pltpu.CompilerParams(vmem_limit_bytes=VMEM_LIMIT),
            cost_estimate=pl.CostEstimate(
                flops=8 * capacity * width * hidden,
                transcendentals=2 * capacity * hidden,
                bytes_accessed=4 * width * hidden,
            ),
            name="experts",
        )(near, far, whole_in, whole_out)

    def combine(where, near, far):
        return small_call(
            combine_kernel,
            [jax.ShapeDtypeStruct((token_rows, width), jnp.bfloat16)],
            4 * capacity * token_rows * width,
            (where, pick, gate, near, far),
        )[0]

    last = planes - 1
    left1 = along(normed, [(i, i + 1) for i in range(last)])
    right1 = along(normed, [(i + 1, i) for i in range(last)])
    left2 = along(left1, [(i, i + 1) for i in range(1, last)])
    right2 = along(right1, [(i + 1, i) for i in range(last - 1)])
    left3 = along(left2, [(2, 3)])
    right3 = along(right2, [(1, 0)])

    upper = (plane >= 2).astype(jnp.int32)

    def where(block):
        return jnp.stack([jnp.clip(block, 0, last), upper]).astype(jnp.int32)

    stages = {
        "own": (plane, (normed,), range(planes)),
        "left": (plane - 1, (left1,), range(1, planes)),
        "right": (plane + 1, (right1,), range(last)),
        "two": (jnp.where(plane >= 2, plane - 2, plane + 2), (left2, right2), range(planes)),
        "three": (last - plane, (left3, right3), (0, last)),
    }
    done = {}
    for name, (block, blocks, on) in stages.items():
        at = where(block)
        near, far = compact(at, blocks)
        came = across(far, on)
        near_done, far_done = experts(near, came)
        back = across(far_done, on)
        done[name] = (at, near_done, back)
    returned = []
    for name, perm in (
        ("left", [(i + 1, i) for i in range(last)]),
        ("right", [(i, i + 1) for i in range(last)]),
        ("two", [(0, 2), (1, 3), (2, 0), (3, 1)]),
        ("three", [(0, last), (last, 0)]),
    ):
        summed = combine(*done[name])
        returned.append(along(summed, perm))
    at, near_done, back = done["own"]
    return small_call(
        final_kernel,
        [jax.ShapeDtypeStruct((token_rows, width), jnp.bfloat16)],
        4 * capacity * token_rows * width,
        (at, pick, gate, near_done, back, residual, modulation, *returned),
    )[0]


def per_device(
    queries, keys, values, tokens, modulation, out_weight, fc_in, fc_out, expert_ids, gate_weights
):
    planes = lax.axis_size("seq")
    heads = queries.shape[1] // HEAD_DIM
    pairs = all(lax.axis_size(a) == 2 for a in ("group", "expert", "fsdp"))
    if pairs and heads % 2 == 0 and heads > planes and 2 * (heads - planes) == planes:
        residual, normed = moved_heads_attention(
            queries, keys, values, tokens, modulation, out_weight
        )
    else:
        residual, normed = gathered_attention(
            queries, keys, values, tokens, modulation, out_weight
        )
    token_rows = tokens.shape[0]
    capacity = 2 * TOP * token_rows // (fc_in.shape[0] * lax.axis_size(("seq", "expert")))
    if (
        planes == 4
        and lax.axis_size("expert") == 2
        and fc_in.shape[0] == 1
        and 2 * capacity >= token_rows
    ):
        return passed_tokens_experts(
            residual, normed, modulation, fc_in, fc_out, expert_ids, gate_weights
        )
    mixture = sent_tokens_experts(normed, fc_in, fc_out, expert_ids, gate_weights)
    return (residual.astype(jnp.float32) + modulation[2] * mixture).astype(jnp.bfloat16)


def solution(mesh):
    placed = (
        P(("group", "seq"), ("expert", "fsdp")),
        P(("group", "seq"), ("expert", "fsdp")),
        P(("group", "seq"), ("expert", "fsdp")),
        P(("group", "seq", "expert", "fsdp"), None),
        P("group", None),
        P(("expert", "fsdp"), None),
        P(("seq", "expert"), "fsdp", None),
        P(("seq", "expert"), "fsdp", None),
        P(("group", "seq", "expert", "fsdp"), None),
        P(("group", "seq", "expert", "fsdp"), None),
    )

    return jax.shard_map(
        per_device,
        mesh=mesh,
        in_specs=placed,
        out_specs=P(("group", "seq", "expert", "fsdp"), None),
        check_vma=False,
    )
```
